32 devices in a mesh: fsdp: 16 (over z, x, core), seq: 2 (over y).
Axes of the slice: x: 2, y: 2, z: 4, core: 2. Of those that a mesh axis runs over, the one named last changes fastest.
Arguments:
- stream: float32 [16, 256, 768], P('fsdp', 'seq'), may hold values from -24 to 24
- encoder: bfloat16 [16, 64, 768], P('fsdp', 'seq'), may hold values from -6 to 6
- self_weights: bfloat16 [3072, 768], P('fsdp'), may hold values from -2 to 2
- cross_weights: bfloat16 [3072, 768], P('fsdp'), may hold values from -2 to 2
- feed_weights: bfloat16 [6144, 768], P('fsdp'), may hold values from -2 to 2
- norm_gains: bfloat16 [3, 768], P(None, 'fsdp'), may hold values from 0.5 to 1.5
- bias_table: float32 [12, 32], replicated, may hold values from -6 to 403
- bucket_onehot: int32 [256, 32], replicated, may hold values from 0 to 1, as said below
- key_keep: int32 [16, 256], P('fsdp'), may hold values 0 or 1
- out_grad: float32 [16, 256, 768], P('fsdp', 'seq'), may hold values from -6 to 6
Outputs:
- output: float32 [16, 256, 768], P('fsdp', 'seq')
- stream_grad: float32 [16, 256, 768], P('fsdp', 'seq')
- encoder_grad: float32 [16, 64, 768], P('fsdp', 'seq')
- gains_grad: float32 [3, 768], replicated
- table_grad: float32 [12, 32], replicated
- self_grad: float32 [3072, 768], P(('fsdp', 'seq'))
- cross_grad: float32 [3072, 768], P(('fsdp', 'seq'))
- feed_grad: float32 [6144, 768], P(('fsdp', 'seq'))
The draws below stay inside these ranges and needn't reach their ends.
Inputs may be any that keep to these rules, and one draw needn't show every extreme that they name: `bucket_onehot`: row r holds a single 1, at the bucket of distance r; bucket numbers never fall as r grows.
All inputs are finite; a program needn't handle non-finite values. No bound on the sum of `key_keep` on one device may be relied on, other than what follows from the above.
Results may differ from the reference program's by a relative error of at most 0.017.
The reference program's roundings to bfloat16 on the way count: a program that leaves them out, or rounds other values in their place, can miss the bound.
Values may be sent and summed in bfloat16 or wider, within the bound.
No kernel may reach another device: no remote copies, remote signals or barrier semaphores. Data moves between devices by JAX's collectives and lax.ppermute only.
A program may use at most 128 MiB of HBM per device.

```python
import math
import jax
import jax.numpy as jnp
from jax import lax

D = 768
H = 12
DK = 64
F = 2048
NB = 32
LEN = 256
ENC = 64
SEQS = 16


def scaled_stack(key, rows_each, factors):
    block_index = jnp.arange(len(factors) * rows_each) // rows_each
    scale_rows = jnp.array(factors, jnp.float32)[block_index]
    base_draw = jnp.clip(jax.random.normal(key, (len(factors) * rows_each, D), jnp.float32), -2.5, 2.5)
    return base_draw * scale_rows[:, None]


def draw_stream(key, part):
    key_base = jax.random.fold_in(key, 11)
    key_rows = jax.random.fold_in(key, 12)
    key_cols = jax.random.fold_in(key, 13)
    base_draw = jnp.clip(jax.random.normal(key_base, (SEQS, LEN, D), jnp.float32), -4.0, 4.0)
    row_scale = jnp.exp(jax.random.uniform(key_rows, (SEQS, LEN, 1), jnp.float32, math.log(0.3), math.log(3.0)))
    col_scale = jnp.exp(jax.random.uniform(key_cols, (1, 1, D), jnp.float32, -0.69, 0.69))
    return base_draw * row_scale * col_scale


def draw_self_weights(key, part):
    return scaled_stack(jax.random.fold_in(key, 71), D, [(D * DK) ** (-0.5), D ** (-0.5), D ** (-0.5), 4.0 * D ** (-0.5)]).astype(jnp.bfloat16)


def draw_cross_weights(key, part):
    return scaled_stack(jax.random.fold_in(key, 72), D, [(D * DK) ** (-0.5), D ** (-0.5), D ** (-0.5), 6.0 * D ** (-0.5)]).astype(jnp.bfloat16)


def draw_feed_weights(key, part):
    return scaled_stack(jax.random.fold_in(key, 73), F, [D ** (-0.5), D ** (-0.5), 2.0 * F ** (-0.5)]).astype(jnp.bfloat16)


def draw_bias_table(key, part):
    key_base = jax.random.fold_in(key, 21)
    return jnp.clip(1.5 * jax.random.normal(key_base, (H, NB), jnp.float32), -6.0, 6.0)


def draw_bucket_onehot(key, part):
    increments = jax.random.randint(jax.random.fold_in(key, 31), (LEN,), 0, 2)
    bucket_ids = jnp.minimum(jnp.cumsum(increments), NB - 1)
    return (bucket_ids[:, None] == jnp.arange(NB)[None, :]).astype(jnp.int32)


def plant(entries, own_key, least, top_value):
    spot = [jax.random.randint(jax.random.fold_in(own_key, axis), (), 0, length) for axis, length in enumerate(entries.shape)]
    longest = entries.shape.index(max(entries.shape))
    next_to = spot[:longest] + [(spot[longest] + 1) % entries.shape[longest]] + spot[longest + 1:]
    return entries.at[tuple(spot)].set(least).at[tuple(next_to)].set(top_value)


def block_levels(key, shape, split, least, largest):
    def one(dim, shards_of):
        heights = jax.random.uniform(jax.random.fold_in(jax.random.fold_in(key, 6), dim), (shards_of,), jnp.float32, least / len(split), largest / len(split))
        return jnp.repeat(jnp.exp(heights), shape[dim] // shards_of).reshape((-1,) + (1,) * (len(shape) - dim - 1))

    level = one(*split[0])
    for cut in split[1:]:
        level = level * one(*cut)
    return level


def scatter_about(rng, extent, scale, reach, pieces=(), kind=jnp.bfloat16):
    level = block_levels(rng, extent, pieces, -0.22, 0.18) if pieces else 1.0
    values = jax.random.normal(rng, extent, jnp.float32) * scale * level
    return jnp.minimum(jnp.maximum(values, -reach), reach).astype(kind)


def setup_inputs(seed: int = 0) -> dict:
    arg_keys = jax.random.split(jax.random.key(seed), 11)
    stream = draw_stream(jax.random.fold_in(arg_keys[10], 71), 0)
    encoder = scatter_about(arg_keys[1], (SEQS, ENC, D), 1.0, 6.0, ((0, 16), (1, 2)))
    self_weights = draw_self_weights(jax.random.fold_in(arg_keys[10], 71), 0)
    cross_weights = draw_cross_weights(jax.random.fold_in(arg_keys[10], 71), 0)
    feed_weights = draw_feed_weights(jax.random.fold_in(arg_keys[10], 71), 0)
    norm_gains = jnp.clip(1.0 + 0.1 * jax.random.normal(arg_keys[5], (3, D), jnp.float32), 0.5, 1.5).astype(jnp.bfloat16)
    bias_table = draw_bias_table(jax.random.fold_in(arg_keys[10], 71), 0)
    bucket_onehot = draw_bucket_onehot(jax.random.fold_in(arg_keys[10], 71), 0)
    key_keep = plant((jax.random.randint(arg_keys[8], (SEQS, LEN), 0, 8) < 7).astype(jnp.int32), jax.random.fold_in(arg_keys[8], 1), 0, 1)
    out_grad = scatter_about(arg_keys[9], (SEQS, LEN, D), 1.0, 6.0, ((0, 16), (1, 2)), jnp.float32)
    return {"stream": stream, "encoder": encoder, "self_weights": self_weights, "cross_weights": cross_weights, "feed_weights": feed_weights, "norm_gains": norm_gains, "bias_table": bias_table, "bucket_onehot": bucket_onehot, "key_keep": key_keep, "out_grad": out_grad}


epsilon = 1e-06
gelu_scale = math.sqrt(2.0 / math.pi)

def rms_norm(rows, gain):
    scale = lax.rsqrt(lax.optimization_barrier(jnp.mean(rows * rows, axis=-1)) + epsilon)
    return ((rows * scale[:, None] * gain).astype(jnp.bfloat16), scale)

def norm_back(rows, scale, gain, dnorm):
    gained = gain * dnorm
    inner = lax.optimization_barrier(jnp.mean(rows * gained, axis=-1, keepdims=True))
    drows = scale[:, None] * gained - rows * (scale ** 3)[:, None] * inner
    dgain = lax.optimization_barrier(jnp.sum(dnorm * rows * scale[:, None], axis=0))
    return (drows, dgain)

def gelu_parts(value):
    tangent = jnp.tanh(gelu_scale * (value + 0.044715 * value * value * value))
    result = 0.5 * value * (1.0 + tangent)
    slope = 0.5 * (1.0 + tangent) + 0.5 * value * (1.0 - tangent * tangent) * gelu_scale * (1.0 + 3.0 * 0.044715 * value * value)
    return (result, slope)

def contract_rows(left, right):
    return lax.dot_general(left, right, (((0,), (0,)), ((), ())), preferred_element_type=jnp.float32)

def contract_cols(left, right):
    return lax.dot_general(left, right, (((1,), (1,)), ((), ())), preferred_element_type=jnp.float32)

def rounded(values):
    return lax.optimization_barrier(values.astype(jnp.bfloat16)).astype(jnp.float32)

def to_heads(values):
    return values.astype(jnp.float32).reshape(values.shape[0], H, DK).transpose(1, 0, 2)

def from_heads(values):
    return values.transpose(1, 0, 2).reshape(values.shape[1], H * DK)

def log_total(scores):
    row_max = lax.optimization_barrier(jnp.max(scores, axis=-1, keepdims=True))
    return row_max + jnp.log(lax.optimization_barrier(jnp.sum(jnp.exp(scores - row_max), axis=-1, keepdims=True)))

def attention_back(queries, key_rows, value_rows, context, totals, context_grad, scores):
    attn_prob = jnp.exp(scores - totals)
    prob_low = rounded(attn_prob)
    grad_heads = to_heads(context_grad)
    row_delta = lax.optimization_barrier(jnp.sum(to_heads(context) * grad_heads, axis=-1, keepdims=True))
    value_grad = jnp.einsum('hqk,hqd->hkd', prob_low, grad_heads)
    prob_grad = jnp.einsum('hqd,hkd->hqk', grad_heads, to_heads(value_rows))
    score_grad = attn_prob * (prob_grad - row_delta)
    score_low = rounded(score_grad)
    query_grad = jnp.einsum('hqk,hkd->hqd', score_low, to_heads(key_rows))
    key_grad = jnp.einsum('hqk,hqd->hkd', score_low, to_heads(queries))
    return (from_heads(query_grad).astype(jnp.bfloat16), from_heads(key_grad).astype(jnp.bfloat16), from_heads(value_grad).astype(jnp.bfloat16), score_grad)

def reference(stream, encoder, self_weights, cross_weights, feed_weights, norm_gains, bias_table, bucket_onehot, key_keep, out_grad):
    gain_rows = norm_gains.astype(jnp.float32)
    self_parts = [self_weights[i * D:(i + 1) * D] for i in range(4)]
    cross_parts = [cross_weights[i * D:(i + 1) * D] for i in range(4)]
    gate_rows = feed_weights[:F]
    up_rows = feed_weights[F:2 * F]
    down_rows = feed_weights[2 * F:]
    onehot = bucket_onehot.astype(jnp.float32)
    dist_bias = jnp.dot(bias_table, onehot.T, precision=lax.Precision.HIGHEST)
    positions = jnp.arange(LEN, dtype=jnp.int32)
    distance = positions[:, None] - positions[None, :]
    dist_index = jnp.clip(distance, 0, LEN - 1).astype(jnp.int32)

    def expand(table_rows):
        return jnp.take(table_rows, dist_index, axis=1)
    bias_full, bias_vjp = jax.vjp(expand, dist_bias)

    def per_sequence(totals, inputs):
        seq_stream, seq_encoder, seq_keep, seq_cotangent = inputs
        norm_one, scale_one = rms_norm(seq_stream, gain_rows[0])
        queries = jnp.dot(norm_one, self_parts[0], preferred_element_type=jnp.float32).astype(jnp.bfloat16)
        key_rows = jnp.dot(norm_one, self_parts[1], preferred_element_type=jnp.float32).astype(jnp.bfloat16)
        value_rows = jnp.dot(norm_one, self_parts[2], preferred_element_type=jnp.float32).astype(jnp.bfloat16)
        allowed = (distance >= 0) & ((seq_keep[None, :] == 1) | (distance == 0))
        self_scores = jnp.einsum('hqd,hkd->hqk', to_heads(queries), to_heads(key_rows)) + bias_full
        self_scores = jnp.where(allowed[None], self_scores, -jnp.inf)
        self_totals = log_total(self_scores)
        self_prob = rounded(jnp.exp(self_scores - self_totals))
        self_context = from_heads(jnp.einsum('hqk,hkd->hqd', self_prob, to_heads(value_rows))).astype(jnp.bfloat16)
        after_self = seq_stream + jnp.dot(self_context, self_parts[3], preferred_element_type=jnp.float32)
        norm_two, scale_two = rms_norm(after_self, gain_rows[1])
        cross_queries = jnp.dot(norm_two, cross_parts[0], preferred_element_type=jnp.float32).astype(jnp.bfloat16)
        cross_keys = jnp.dot(seq_encoder, cross_parts[1], preferred_element_type=jnp.float32).astype(jnp.bfloat16)
        cross_values = jnp.dot(seq_encoder, cross_parts[2], preferred_element_type=jnp.float32).astype(jnp.bfloat16)
        cross_scores = jnp.einsum('hqd,hkd->hqk', to_heads(cross_queries), to_heads(cross_keys))
        cross_totals = log_total(cross_scores)
        cross_prob = rounded(jnp.exp(cross_scores - cross_totals))
        cross_context = from_heads(jnp.einsum('hqk,hkd->hqd', cross_prob, to_heads(cross_values))).astype(jnp.bfloat16)
        after_cross = after_self + jnp.dot(cross_context, cross_parts[3], preferred_element_type=jnp.float32)
        norm_three, scale_three = rms_norm(after_cross, gain_rows[2])
        gate_pre = contract_cols(norm_three, gate_rows)
        up_pre = contract_cols(norm_three, up_rows)
        gate_act, gate_slope = gelu_parts(gate_pre)
        hidden = (gate_act * up_pre).astype(jnp.bfloat16)
        output = after_cross + jnp.dot(hidden, down_rows, preferred_element_type=jnp.float32)
        cot_low = seq_cotangent.astype(jnp.bfloat16)
        down_wgrad = contract_rows(hidden, cot_low)
        hidden_grad = contract_cols(cot_low, down_rows)
        gate_grad = (hidden_grad * up_pre * gate_slope).astype(jnp.bfloat16)
        up_grad = (hidden_grad * gate_act).astype(jnp.bfloat16)
        gate_wgrad = contract_rows(gate_grad, norm_three)
        up_wgrad = contract_rows(up_grad, norm_three)
        norm_three_grad = jnp.dot(gate_grad, gate_rows, preferred_element_type=jnp.float32) + jnp.dot(up_grad, up_rows, preferred_element_type=jnp.float32)
        stream_three, gain_three = norm_back(after_cross, scale_three, gain_rows[2], norm_three_grad)
        cross_in_grad = seq_cotangent + stream_three
        cross_low = cross_in_grad.astype(jnp.bfloat16)
        cross_out_wgrad = contract_rows(cross_context, cross_low)
        cross_context_grad = contract_cols(cross_low, cross_parts[3]).astype(jnp.bfloat16)
        cross_qgrad, cross_kgrad, cross_vgrad, unused_grad = attention_back(cross_queries, cross_keys, cross_values, cross_context, cross_totals, cross_context_grad, cross_scores)
        norm_two_grad = contract_cols(cross_qgrad, cross_parts[0])
        encoder_grad = contract_cols(cross_kgrad, cross_parts[1]) + contract_cols(cross_vgrad, cross_parts[2])
        cross_wgrad = jnp.concatenate([contract_rows(norm_two, cross_qgrad), contract_rows(seq_encoder, cross_kgrad), contract_rows(seq_encoder, cross_vgrad), cross_out_wgrad], axis=0)
        stream_two, gain_two = norm_back(after_self, scale_two, gain_rows[1], norm_two_grad)
        self_in_grad = cross_in_grad + stream_two
        self_low = self_in_grad.astype(jnp.bfloat16)
        self_out_wgrad = contract_rows(self_context, self_low)
        self_context_grad = contract_cols(self_low, self_parts[3]).astype(jnp.bfloat16)
        self_qgrad, self_kgrad, self_vgrad, self_score_grad = attention_back(queries, key_rows, value_rows, self_context, self_totals, self_context_grad, self_scores)
        dist_grad = bias_vjp(self_score_grad)[0]
        table_grad = jnp.dot(dist_grad, onehot, precision=lax.Precision.HIGHEST)
        norm_one_grad = contract_cols(self_qgrad, self_parts[0]) + contract_cols(self_kgrad, self_parts[1]) + contract_cols(self_vgrad, self_parts[2])
        stream_one, gain_one = norm_back(seq_stream, scale_one, gain_rows[0], norm_one_grad)
        stream_grad = self_in_grad + stream_one
        self_wgrad = jnp.concatenate([contract_rows(norm_one, self_qgrad), contract_rows(norm_one, self_kgrad), contract_rows(norm_one, self_vgrad), self_out_wgrad], axis=0)
        feed_wgrad = jnp.concatenate([gate_wgrad, up_wgrad, down_wgrad], axis=0)
        gain_grads = jnp.stack([gain_one, gain_two, gain_three])
        totals = (totals[0] + gain_grads, totals[1] + table_grad, totals[2] + self_wgrad, totals[3] + cross_wgrad, totals[4] + feed_wgrad)
        return (totals, (output, stream_grad, encoder_grad))
    start_totals = (jnp.zeros((3, D), jnp.float32), jnp.zeros((H, NB), jnp.float32), jnp.zeros((4 * D, D), jnp.float32), jnp.zeros((4 * D, D), jnp.float32), jnp.zeros((3 * F, D), jnp.float32))
    totals, results = lax.scan(per_sequence, start_totals, (stream, encoder, key_keep, out_grad))
    return (results[0], results[1], results[2], totals[0], totals[1], totals[2], totals[3], totals[4])
```

```python
import functools
import math

import jax
import jax.numpy as jnp
import numpy as np
from jax import lax
from jax.experimental import pallas as pl
from jax.experimental.pallas import tpu as pltpu
from jax.sharding import PartitionSpec as P

H = 12
DK = 64
F = 2048
EPS = 1e-06
GELU_SCALE = math.sqrt(2.0 / math.pi)
BF = jnp.bfloat16
F32 = jnp.float32
VMEM_SPEC = pl.BlockSpec(memory_space=pltpu.VMEM)
SMEM_SPEC = pl.BlockSpec(memory_space=pltpu.SMEM)
PARAMS = pltpu.CompilerParams(vmem_limit_bytes=56 * 1024 * 1024)


def dot_nn(a, b):
    return lax.dot_general(a, b, (((1,), (0,)), ((), ())), preferred_element_type=F32)


def dot_nt(a, b):
    return lax.dot_general(a, b, (((1,), (1,)), ((), ())), preferred_element_type=F32)


def dot_tn(a, b):
    return lax.dot_general(a, b, (((0,), (0,)), ((), ())), preferred_element_type=F32)


def rms_scale(rows):
    return lax.rsqrt(jnp.mean(rows * rows, axis=-1, keepdims=True) + EPS)


def norm_back(rows, gain, dnorm):
    scale = rms_scale(rows)
    gained = gain * dnorm
    inner = jnp.mean(rows * gained, axis=-1, keepdims=True)
    drows = scale * gained - rows * (scale * scale * scale) * inner
    dgain = jnp.sum(dnorm * rows * scale, axis=0, keepdims=True)
    return drows, dgain


def half_masks():
    lane = lax.broadcasted_iota(jnp.int32, (1, 2 * DK), 1)
    low = jnp.where(lane < DK, 1.0, 0.0)
    return low.astype(F32), (1.0 - low).astype(F32)


def softmax_rows(scores):
    row_max = jnp.max(scores, axis=-1, keepdims=True)
    expd = jnp.exp(scores - row_max)
    return expd / jnp.sum(expd, axis=-1, keepdims=True)


def qkv_kernel(stream_ref, gain_ref, w_ref, q_ref, kv_ref, n1t_ref, norm_ref):
    step = pl.program_id(0)

    @pl.when(step == 0)
    def _():
        rows = stream_ref[...]
        normed = rows * rms_scale(rows) * gain_ref[0:1]
        norm_ref[...] = normed.astype(BF)
        n1t_ref[...] = normed.T.astype(BF)

    out = dot_nn(norm_ref[...], w_ref[...]).astype(BF)

    @pl.when(step == 0)
    def _():
        q_ref[...] = out

    @pl.when(step > 0)
    def _():
        kv_ref[0] = out


def run_qkv(stream, gains, self_full):
    tokens, features = stream.shape
    return pl.pallas_call(
        qkv_kernel,
        grid=(3,),
        in_specs=[
            pl.BlockSpec((tokens, features), lambda i: (0, 0)),
            pl.BlockSpec((3, features), lambda i: (0, 0)),
            pl.BlockSpec((features, features), lambda i: (i, 0)),
        ],
        out_specs=[
            pl.BlockSpec((tokens, features), lambda i: (0, 0)),
            pl.BlockSpec((1, tokens, features), lambda i: (jnp.maximum(i - 1, 0), 0, 0)),
            pl.BlockSpec((features, tokens), lambda i: (0, 0)),
        ],
        out_shape=[
            jax.ShapeDtypeStruct((tokens, features), BF),
            jax.ShapeDtypeStruct((2, tokens, features), BF),
            jax.ShapeDtypeStruct((features, tokens), BF),
        ],
        scratch_shapes=[pltpu.VMEM((tokens, features), BF)],
        compiler_params=PARAMS,
        name="qkv",
    )(stream, gains, self_full)


def join_pieces(own, others, which):
    return jnp.concatenate([own[which]] + [piece[which] for piece in others], axis=0)


def self_fwd_kernel(group_size, *refs):
    pos_ref, q_ref, kv_ref = refs[:3]
    other_refs = refs[3 : 2 + group_size]
    keep_ref, bias_ref, stream_ref, w_ref, gain_ref = refs[2 + group_size : 7 + group_size]
    prob_ref, ctx_ref, ctxt_ref, after_ref, n2_ref, n2t_ref = refs[7 + group_size :]
    tokens = q_ref.shape[0]
    total = tokens * group_size
    pos = pos_ref[0]
    keys = join_pieces(kv_ref, other_refs, 0)
    values = join_pieces(kv_ref, other_refs, 1)
    row = lax.broadcasted_iota(jnp.int32, (tokens, total), 0)
    col = lax.broadcasted_iota(jnp.int32, (tokens, total), 1)
    keep = jnp.broadcast_to(keep_ref[...], (tokens, total)) > 0
    earlier = (col >= tokens) & (pos * tokens + col >= total)
    allowed = (col == row) | (keep & ((col < row) | earlier))
    masks = half_masks()
    lane_low = lax.broadcasted_iota(jnp.int32, (tokens, 2 * DK), 1) < DK
    for pair in range(H // 2):
        cols = slice(pair * 2 * DK, (pair + 1) * 2 * DK)
        query_pair = q_ref[:, cols]
        key_pair = keys[:, cols]
        value_pair = values[:, cols]
        parts = []
        for half in range(2):
            head = pair * 2 + half
            scores = dot_nt(query_pair * masks[half].astype(BF), key_pair)
            line = jnp.broadcast_to(bias_ref[head : head + 1, :], (tokens, total))
            scores = scores + pltpu.roll(line, 0, 1, stride=1, stride_axis=0)
            prob = softmax_rows(jnp.where(allowed, scores, -jnp.inf))
            prob_ref[head] = prob
            parts.append(dot_nn(prob.astype(BF), value_pair))
        ctx_pair = jnp.where(lane_low, parts[0], parts[1])
        ctx_ref[:, cols] = ctx_pair.astype(BF)
        ctxt_ref[cols, :] = ctx_pair.T.astype(BF)
    after = stream_ref[...] + dot_nn(ctx_ref[...], w_ref[...])
    after_ref[...] = after
    normed = after * rms_scale(after) * gain_ref[1:2]
    n2_ref[...] = normed.astype(BF)
    n2t_ref[...] = normed.T.astype(BF)


def run_self_fwd(pos, q, kv, others, keep, bias_line, stream, self_full, gains):
    tokens, features = stream.shape
    group_size = len(others) + 1
    total = tokens * group_size
    return pl.pallas_call(
        functools.partial(self_fwd_kernel, group_size),
        grid=(1,),
        in_specs=[SMEM_SPEC, VMEM_SPEC, VMEM_SPEC]
        + [VMEM_SPEC] * len(others)
        + [VMEM_SPEC, VMEM_SPEC, VMEM_SPEC]
        + [pl.BlockSpec((features, features), lambda i: (3, 0)), VMEM_SPEC],
        out_specs=[VMEM_SPEC] * 6,
        out_shape=[
            jax.ShapeDtypeStruct((H, tokens, total), F32),
            jax.ShapeDtypeStruct((tokens, features), BF),
            jax.ShapeDtypeStruct((features, tokens), BF),
            jax.ShapeDtypeStruct((tokens, features), F32),
            jax.ShapeDtypeStruct((tokens, features), BF),
            jax.ShapeDtypeStruct((features, tokens), BF),
        ],
        compiler_params=PARAMS,
        name="self_fwd",
    )(pos, q, kv, *others, keep, bias_line, stream, self_full, gains)


def cross_fwd_kernel(
    after_ref, n2_ref, enc_ref, w_ref, gain_ref,
    prob_ref, cq_ref, ckv_ref, ctx_ref, ctxt_ref, out_ref, n3_ref,
):
    tokens, features = n2_ref.shape
    cq_ref[...] = dot_nn(n2_ref[...], w_ref[0:features]).astype(BF)
    ckv_ref[0] = dot_nn(enc_ref[...], w_ref[features : 2 * features]).astype(BF)
    ckv_ref[1] = dot_nn(enc_ref[...], w_ref[2 * features : 3 * features]).astype(BF)
    masks = half_masks()
    lane_low = lax.broadcasted_iota(jnp.int32, (tokens, 2 * DK), 1) < DK
    for pair in range(H // 2):
        cols = slice(pair * 2 * DK, (pair + 1) * 2 * DK)
        query_pair = cq_ref[:, cols]
        key_pair = ckv_ref[0, :, cols]
        value_pair = ckv_ref[1, :, cols]
        parts = []
        for half in range(2):
            scores = dot_nt(query_pair * masks[half].astype(BF), key_pair)
            prob = softmax_rows(scores)
            prob_ref[pair * 2 + half] = prob
            parts.append(dot_nn(prob.astype(BF), value_pair))
        ctx_pair = jnp.where(lane_low, parts[0], parts[1])
        ctx_ref[:, cols] = ctx_pair.astype(BF)
        ctxt_ref[cols, :] = ctx_pair.T.astype(BF)
    after = after_ref[...] + dot_nn(ctx_ref[...], w_ref[3 * features : 4 * features])
    out_ref[...] = after
    n3_ref[...] = (after * rms_scale(after) * gain_ref[2:3]).astype(BF)


def run_cross_fwd(after_self, n2, enc_all, cross_full, gains):
    tokens, features = after_self.shape
    enc_len = enc_all.shape[0]
    return pl.pallas_call(
        cross_fwd_kernel,
        in_specs=[VMEM_SPEC] * 5,
        out_specs=[VMEM_SPEC] * 7,
        out_shape=[
            jax.ShapeDtypeStruct((H, tokens, enc_len), F32),
            jax.ShapeDtypeStruct((tokens, features), BF),
            jax.ShapeDtypeStruct((2, enc_len, features), BF),
            jax.ShapeDtypeStruct((tokens, features), BF),
            jax.ShapeDtypeStruct((features, tokens), BF),
            jax.ShapeDtypeStruct((tokens, features), F32),
            jax.ShapeDtypeStruct((tokens, features), BF),
        ],
        compiler_params=PARAMS,
        name="cross_fwd",
    )(after_self, n2, enc_all, cross_full, gains)


def gelu_parts(value):
    tangent = jnp.tanh(GELU_SCALE * (value + 0.044715 * value * value * value))
    result = 0.5 * value * (1.0 + tangent)
    slope = 0.5 * (1.0 + tangent) + 0.5 * value * (1.0 - tangent * tangent) * GELU_SCALE * (
        1.0 + 3.0 * 0.044715 * value * value
    )
    return result, slope


def feed_kernel(
    n3_ref, grad_ref, after_ref, gain_ref, g0_ref, g1_ref, g2_ref,
    hgu_ref, out_ref, in_grad_ref, dgain_ref, cot_ref, acc_ref,
):
    step = pl.program_id(0)
    last = pl.num_programs(0) - 1

    @pl.when(step == 0)
    def _():
        cot_ref[...] = grad_ref[...].astype(BF)
        out_ref[...] = after_ref[...]
        acc_ref[...] = jnp.zeros_like(acc_ref)

    n3 = n3_ref[...]
    gate_pre = dot_nt(g0_ref[...], n3)
    up_pre = dot_nt(g1_ref[...], n3)
    hidden_grad = dot_nt(g2_ref[...], cot_ref[...])
    gate_act, gate_slope = gelu_parts(gate_pre)
    hidden = (gate_act * up_pre).astype(BF)
    gate_grad = (hidden_grad * up_pre * gate_slope).astype(BF)
    up_grad = (hidden_grad * gate_act).astype(BF)
    hgu_ref[0] = gate_grad
    hgu_ref[1] = up_grad
    hgu_ref[2] = hidden
    out_ref[...] += dot_tn(hidden, g2_ref[...])
    acc_ref[...] += dot_tn(gate_grad, g0_ref[...]) + dot_tn(up_grad, g1_ref[...])

    @pl.when(step == last)
    def _():
        drows, dgain = norm_back(after_ref[...], gain_ref[2:3], acc_ref[...])
        in_grad_ref[...] = grad_ref[...] + drows
        dgain_ref[...] = dgain


def run_feed(n3, out_grad, after_cross, gains, feed_full):
    tokens, features = out_grad.shape
    block = 256
    steps = F // block
    whole = pl.BlockSpec((tokens, features), lambda i: (0, 0))
    return pl.pallas_call(
        feed_kernel,
        grid=(steps,),
        in_specs=[
            whole,
            whole,
            whole,
            pl.BlockSpec((3, features), lambda i: (0, 0)),
            pl.BlockSpec((block, features), lambda i: (i, 0)),
            pl.BlockSpec((block, features), lambda i: (i + steps, 0)),
            pl.BlockSpec((block, features), lambda i: (i + 2 * steps, 0)),
        ],
        out_specs=[
            pl.BlockSpec((3, block, tokens), lambda i: (0, i, 0)),
            whole,
            whole,
            pl.BlockSpec((1, features), lambda i: (0, 0)),
        ],
        out_shape=[
            jax.ShapeDtypeStruct((3, F, tokens), BF),
            jax.ShapeDtypeStruct((tokens, features), F32),
            jax.ShapeDtypeStruct((tokens, features), F32),
            jax.ShapeDtypeStruct((1, features), F32),
        ],
        scratch_shapes=[pltpu.VMEM((tokens, features), BF), pltpu.VMEM((tokens, features), F32)],
        compiler_params=PARAMS,
        name="feed",
    )(n3, out_grad, after_cross, gains, feed_full, feed_full, feed_full)


def cross_bwd_kernel(
    in_grad_ref, w_ref, prob_ref, ctx_ref, cq_ref, ckv_ref, after_ref, gain_ref,
    pack_ref, enc_pack_ref, out_ref, dgain_ref,
):
    tokens, features = cq_ref.shape
    low = in_grad_ref[...].astype(BF)
    pack_ref[0] = low
    ctx_grad = dot_nt(low, w_ref[3 * features : 4 * features]).astype(BF)
    masks = half_masks()
    lane_low = lax.broadcasted_iota(jnp.int32, (tokens, 2 * DK), 1) < DK
    enc_low = lax.broadcasted_iota(jnp.int32, (ckv_ref.shape[1], 2 * DK), 1) < DK
    for pair in range(H // 2):
        cols = slice(pair * 2 * DK, (pair + 1) * 2 * DK)
        grad_pair = ctx_grad[:, cols]
        query_pair = cq_ref[:, cols]
        key_pair = ckv_ref[0, :, cols]
        value_pair = ckv_ref[1, :, cols]
        weighted = ctx_ref[:, cols].astype(F32) * grad_pair.astype(F32)
        dq, dk, dv = [], [], []
        for half in range(2):
            prob = prob_ref[pair * 2 + half]
            delta = jnp.sum(weighted * masks[half], axis=-1, keepdims=True)
            prob_grad = dot_nt(grad_pair * masks[half].astype(BF), value_pair)
            score_low = (prob * (prob_grad - delta)).astype(BF)
            dq.append(dot_nn(score_low, key_pair))
            dk.append(dot_tn(score_low, query_pair))
            dv.append(dot_tn(prob.astype(BF), grad_pair))
        pack_ref[1, :, cols] = jnp.where(lane_low, dq[0], dq[1]).astype(BF)
        enc_pack_ref[0, :, cols] = jnp.where(enc_low, dk[0], dk[1]).astype(BF)
        enc_pack_ref[1, :, cols] = jnp.where(enc_low, dv[0], dv[1]).astype(BF)
    n2_grad = dot_nt(pack_ref[1], w_ref[0:features])
    drows, dgain = norm_back(after_ref[...], gain_ref[1:2], n2_grad)
    self_in = in_grad_ref[...] + drows
    out_ref[...] = self_in
    pack_ref[2] = self_in.astype(BF)
    dgain_ref[...] = dgain


def run_cross_bwd(in_grad, cross_full, prob, ctx, cq, ckv, after_self, gains):
    tokens, features = in_grad.shape
    return pl.pallas_call(
        cross_bwd_kernel,
        in_specs=[VMEM_SPEC] * 8,
        out_specs=[VMEM_SPEC] * 4,
        out_shape=[
            jax.ShapeDtypeStruct((3, tokens, features), BF),
            jax.ShapeDtypeStruct(ckv.shape, BF),
            jax.ShapeDtypeStruct((tokens, features), F32),
            jax.ShapeDtypeStruct((1, features), F32),
        ],
        compiler_params=PARAMS,
        name="cross_bwd",
    )(in_grad, cross_full, prob, ctx, cq, ckv, after_self, gains)


def unskew(grid):
    tokens, total = grid.shape
    row = lax.broadcasted_iota(jnp.int32, (tokens, total), 0)
    step = 1
    while step < tokens:
        moved = pltpu.roll(grid, total - step, 1)
        grid = jnp.where((row & step) != 0, moved, grid)
        step *= 2
    return jnp.sum(grid, axis=0, keepdims=True)


def self_bwd_kernel(group_size, *refs):
    low_ref, w_ref, prob_ref, ctx_ref, q_ref, kv_ref = refs[:6]
    other_refs = refs[6 : 5 + group_size]
    pack_ref, dist_ref = refs[5 + group_size :]
    tokens = q_ref.shape[0]
    ctx_grad = dot_nt(low_ref[0], w_ref[...]).astype(BF)
    keys = join_pieces(kv_ref, other_refs, 0)
    values = join_pieces(kv_ref, other_refs, 1)
    masks = half_masks()
    lane_low = lax.broadcasted_iota(jnp.int32, (tokens, 2 * DK), 1) < DK
    key_low = lax.broadcasted_iota(jnp.int32, (tokens * group_size, 2 * DK), 1) < DK
    for pair in range(H // 2):
        cols = slice(pair * 2 * DK, (pair + 1) * 2 * DK)
        grad_pair = ctx_grad[:, cols]
        query_pair = q_ref[:, cols]
        key_pair = keys[:, cols]
        value_pair = values[:, cols]
        weighted = ctx_ref[:, cols].astype(F32) * grad_pair.astype(F32)
        dq, dk, dv = [], [], []
        for half in range(2):
            head = pair * 2 + half
            prob = prob_ref[head]
            delta = jnp.sum(weighted * masks[half], axis=-1, keepdims=True)
            prob_grad = dot_nt(grad_pair * masks[half].astype(BF), value_pair)
            score_grad = prob * (prob_grad - delta)
            dist_ref[head : head + 1, :] = unskew(score_grad)
            score_low = score_grad.astype(BF)
            dq.append(dot_nn(score_low, key_pair))
            dk.append(dot_tn(score_low, query_pair))
            dv.append(dot_tn(prob.astype(BF), grad_pair))
        pack_ref[0, :, cols] = jnp.where(lane_low, dq[0], dq[1]).astype(BF)
        dk_pair = jnp.where(key_low, dk[0], dk[1]).astype(BF)
        dv_pair = jnp.where(key_low, dv[0], dv[1]).astype(BF)
        for piece in range(group_size):
            rows = slice(piece * tokens, (piece + 1) * tokens)
            pack_ref[1 + piece, :, cols] = dk_pair[rows]
            pack_ref[1 + group_size + piece, :, cols] = dv_pair[rows]


def run_self_bwd(cross_pack, self_full, prob, ctx, q, kv, others):
    tokens, features = q.shape
    group_size = len(others) + 1
    return pl.pallas_call(
        functools.partial(self_bwd_kernel, group_size),
        grid=(1,),
        in_specs=[
            pl.BlockSpec((1, tokens, features), lambda i: (2, 0, 0)),
            pl.BlockSpec((features, features), lambda i: (3, 0)),
        ]
        + [VMEM_SPEC] * (3 + group_size),
        out_specs=[VMEM_SPEC] * 2,
        out_shape=[
            jax.ShapeDtypeStruct((1 + 2 * group_size, tokens, features), BF),
            jax.ShapeDtypeStruct((H, tokens * group_size), F32),
        ],
        compiler_params=PARAMS,
        name="self_bwd",
    )(cross_pack, self_full, prob, ctx, q, kv, *others)


def qkv_bwd_kernel(group_size, *refs):
    pack_refs = refs[:group_size]
    w_ref, stream_ref, gain_ref, in_grad_ref = refs[group_size : group_size + 4]
    sums_ref, out_ref, dgain_ref, acc_ref = refs[group_size + 4 :]
    step = pl.program_id(0)

    @pl.when(step == 0)
    def _():
        for source in range(group_size):
            sums_ref[0, source] = pack_refs[source][0]
        acc_ref[...] = dot_nt(pack_refs[0][0], w_ref[...])

    @pl.when(step > 0)
    def _():
        base = 1 + (step - 1) * group_size
        for piece in range(group_size):
            total = None
            for source in range(group_size):
                part = pack_refs[source][base + (piece - source) % group_size].astype(F32)
                total = part if total is None else total + part
            sums_ref[0, piece] = total.astype(BF)
        acc_ref[...] += dot_nt(sums_ref[0, 0], w_ref[...])

    @pl.when(step == 2)
    def _():
        drows, dgain = norm_back(stream_ref[...], gain_ref[0:1], acc_ref[...])
        out_ref[...] = in_grad_ref[...] + drows
        dgain_ref[...] = dgain


def run_qkv_bwd(packs, self_full, stream, gains, self_in_grad):
    tokens, features = stream.shape
    group_size = len(packs)
    whole = pl.BlockSpec((tokens, features), lambda i: (0, 0))
    pack_spec = pl.BlockSpec((1 + 2 * group_size, tokens, features), lambda i: (0, 0, 0))
    return pl.pallas_call(
        functools.partial(qkv_bwd_kernel, group_size),
        grid=(3,),
        in_specs=[pack_spec] * group_size
        + [
            pl.BlockSpec((features, features), lambda i: (i, 0)),
            whole,
            pl.BlockSpec((3, features), lambda i: (0, 0)),
            whole,
        ],
        out_specs=[
            pl.BlockSpec((1, group_size, tokens, features), lambda i: (i, 0, 0, 0)),
            whole,
            pl.BlockSpec((1, features), lambda i: (0, 0)),
        ],
        out_shape=[
            jax.ShapeDtypeStruct((3, group_size, tokens, features), BF),
            jax.ShapeDtypeStruct((tokens, features), F32),
            jax.ShapeDtypeStruct((1, features), F32),
        ],
        scratch_shapes=[pltpu.VMEM((tokens, features), F32)],
        compiler_params=PARAMS,
        name="qkv_bwd",
    )(*packs, self_full, stream, gains, self_in_grad)


def feed_wgrad_kernel(group_size, split, owner_ref, *refs):
    hgu_refs = refs[:group_size]
    n3_refs = refs[group_size : 2 * group_size]
    cot_refs = refs[2 * group_size : 3 * group_size]
    out_ref = refs[3 * group_size]
    rows = out_ref.shape[1]
    start = (owner_ref[pl.program_id(0)] * group_size + owner_ref[pl.num_programs(0)]) * rows

    def product(right_refs, mask):
        total = None
        for left_ref, right_ref in zip(hgu_refs, right_refs):
            left = left_ref[...].reshape(rows, left_ref.shape[-1])
            if mask is not None:
                left = left * mask
            part = dot_nn(left, right_ref[...])
            total = part if total is None else total + part
        return total

    @pl.when(start + rows <= split)
    def _():
        out_ref[0] = product(n3_refs, None).astype(BF)

    @pl.when(start >= split)
    def _():
        out_ref[0] = product(cot_refs, None).astype(BF)

    @pl.when((start < split) & (start + rows > split))
    def _():
        row = start + lax.broadcasted_iota(jnp.int32, (rows, 1), 0)
        early = jnp.where(row < split, 1.0, 0.0).astype(F32)
        out_ref[0] = (
            product(n3_refs, None) * early + product(cot_refs, None) * (1.0 - early)
        ).astype(BF)


def run_feed_wgrad(owners, hgu, hgu_others, n3s, cots, rows):
    group_size = len(n3s)
    tokens, features = n3s[0].shape
    count = owners.shape[0] - 1
    whole = pl.BlockSpec((tokens, features), lambda i, o: (0, 0))
    return pl.pallas_call(
        functools.partial(feed_wgrad_kernel, group_size, 2 * F),
        grid_spec=pltpu.PrefetchScalarGridSpec(
            num_scalar_prefetch=1,
            grid=(count,),
            in_specs=[pl.BlockSpec((1, 1, rows, tokens), lambda i, o: (o[i], o[count], 0, 0))]
            + [pl.BlockSpec((1, rows, tokens), lambda i, o: (o[i], 0, 0))] * (group_size - 1)
            + [whole] * (2 * group_size),
            out_specs=pl.BlockSpec((1, rows, features), lambda i, o: (i, 0, 0)),
        ),
        out_shape=jax.ShapeDtypeStruct((count, rows, features), BF),
        compiler_params=PARAMS,
        name="feed_wgrad",
    )(owners, hgu, *hgu_others, *n3s, *cots)


def attn_wgrad_kernel(group_size, per_matrix, picks, owner_ref, *refs):
    out_ref = refs[-1]
    owner = owner_ref[pl.program_id(0)]
    matrix = owner // per_matrix
    block = owner % per_matrix
    for index, (lefts, rights) in enumerate(picks):

        @pl.when(matrix == index)
        def _():
            total = None
            for (left, piece), (right, where) in zip(lefts, rights):
                left_ref, right_ref = refs[left], refs[right]
                left_rows = left_ref[block] if piece is None else left_ref[block, owner_ref[pl.num_programs(0)]]
                part = dot_nn(left_rows, right_ref[where])
                total = part if total is None else total + part
            out_ref[0] = total.astype(BF)


def run_attn_wgrad(owners, picks, arrays, group_size, per_matrix, rows, features):
    count = owners.shape[0] - 1
    return pl.pallas_call(
        functools.partial(attn_wgrad_kernel, group_size, per_matrix, picks),
        grid_spec=pltpu.PrefetchScalarGridSpec(
            num_scalar_prefetch=1,
            grid=(count,),
            in_specs=[
                pl.BlockSpec(array.shape, lambda i, o, rank=array.ndim: (0,) * rank)
                for array in arrays
            ],
            out_specs=pl.BlockSpec((1, rows, features), lambda i, o: (i, 0, 0)),
        ),
        out_shape=jax.ShapeDtypeStruct((count, rows, features), BF),
        compiler_params=PARAMS,
        name="attn_wgrad",
    )(owners, *arrays)


def bit_reverse(value, bits):
    return int(format(value, f"0{bits}b")[::-1], 2) if bits else 0


def local(
    stream, encoder, self_weights, cross_weights, feed_weights,
    norm_gains, bias_table, bucket_onehot, key_keep, out_grad,
):
    group_size = lax.axis_size("seq")
    group_pos = lax.axis_index("seq")
    shard_count = lax.axis_size("fsdp")
    shard_pos = lax.axis_index("fsdp")
    shard_bits = shard_count.bit_length() - 1
    seq_count, tokens, features = stream.shape
    assert seq_count == 1
    enc_piece = encoder.shape[1]
    enc_len = enc_piece * group_size
    full_len = tokens * group_size
    per_matrix = shard_count // 4
    attn_rows = self_weights.shape[0] // group_size
    feed_rows = feed_weights.shape[0] // group_size

    stream = stream[0]
    out_grad = out_grad[0]
    encoder = encoder[0]

    def from_peer(values, offset):
        return lax.ppermute(
            values, "seq", [(i, (i - offset) % group_size) for i in range(group_size)]
        )

    def exchange(values):
        return [from_peer(values, d) for d in range(1, group_size)]

    def exchange_rows(values):
        return [
            from_peer(
                lax.dynamic_index_in_dim(values, (group_pos - d) % group_size, 1, keepdims=False), d
            )
            for d in range(1, group_size)
        ]

    enc_all = lax.dynamic_update_slice_in_dim(
        jnp.zeros((enc_len, features), BF), encoder, group_pos * enc_piece, 0
    )
    for d, piece in enumerate(exchange(encoder), 1):
        enc_all = lax.dynamic_update_slice_in_dim(
            enc_all, piece, ((group_pos + d) % group_size) * enc_piece, 0
        )
    cot_low = out_grad.astype(BF)
    cots = [cot_low] + exchange(cot_low)

    self_full = lax.all_gather(self_weights, "fsdp", axis=0, tiled=True)
    gains = lax.all_gather(norm_gains, "fsdp", axis=1, tiled=True).astype(F32)
    cross_full = lax.all_gather(cross_weights, "fsdp", axis=0, tiled=True)
    feed_full = lax.all_gather(feed_weights, "fsdp", axis=0, tiled=True)

    onehot = bucket_onehot.astype(F32)
    onehot_line = jnp.concatenate([onehot[:1], jnp.flip(onehot[1:], axis=0)], axis=0)
    bias_line = lax.dot_general(
        bias_table, onehot_line, (((1,), (1,)), ((), ())), precision=lax.Precision.HIGHEST
    )
    keep = key_keep.astype(F32)
    keep = lax.dynamic_slice_in_dim(
        jnp.concatenate([keep, keep], axis=1), group_pos * tokens, full_len, 1
    )
    pos = group_pos.astype(jnp.int32)[None]

    q, kv, n1t = run_qkv(stream, gains, self_full)
    kv_others = exchange(kv)
    prob, ctx, ctxt, after_self, n2, n2t = run_self_fwd(
        pos, q, kv, kv_others, keep, bias_line, stream, self_full, gains
    )
    cross_prob, cq, ckv, cctx, cctxt, after_cross, n3 = run_cross_fwd(
        after_self, n2, enc_all, cross_full, gains
    )

    def blocks(values):
        return values.reshape(-1, group_size, attn_rows, values.shape[-1])

    lefts = jnp.stack([blocks(n1t), blocks(ctxt), blocks(n2t), blocks(cctxt)])
    lefts = lefts.reshape(4 * per_matrix, group_size, attn_rows, tokens)
    left_others = exchange_rows(lefts)
    n3s = [n3] + exchange(n3)

    hgu, output, cross_in_grad, gain_three = run_feed(n3, out_grad, after_cross, gains, feed_full)
    hgu = hgu.reshape(shard_count, group_size, feed_rows, tokens)
    hgu_others = exchange_rows(hgu)

    order = [bit_reverse(p, shard_bits) for p in range(shard_count)]
    owners = jnp.array(order, jnp.int32) ^ shard_pos.astype(jnp.int32)
    half = shard_count // 2
    owners_keep = jnp.concatenate([owners[:half], pos])
    owners_send = jnp.concatenate([owners[half:], pos])

    def swap(values, bit):
        return lax.ppermute(values, "fsdp", [(i, i ^ (1 << bit)) for i in range(shard_count)])

    def scatter_sum(product):
        got = swap(product(owners_send), 0)
        kept = product(owners_keep)
        for bit in range(1, shard_bits):
            size = kept.shape[0] // 2
            send = (kept[size:].astype(F32) + got[size:].astype(F32)).astype(BF)
            moved = swap(send, bit)
            kept = kept[:size].astype(F32) + got[:size].astype(F32)
            got = moved
        return (kept.astype(F32) + got.astype(F32))[0]

    feed_grad = scatter_sum(
        lambda owners: run_feed_wgrad(owners, hgu, hgu_others, n3s, cots, feed_rows)
    )

    cross_pack, enc_pack, self_in_grad, gain_two = run_cross_bwd(
        cross_in_grad, cross_full, cross_prob, cctx, cq, ckv, after_self, gains
    )
    cross_others = exchange(cross_pack)
    enc_sum = enc_pack.astype(F32)
    for piece in exchange(enc_pack):
        enc_sum = enc_sum + piece.astype(F32)
    enc_sum = enc_sum.astype(BF)

    self_pack, dist_grad = run_self_bwd(cross_pack, self_full, prob, ctx, q, kv, kv_others)
    self_others = exchange(self_pack)

    def own_rows(values):
        return lax.dynamic_index_in_dim(values, group_pos, 1, keepdims=False)

    left_own = own_rows(lefts)
    left_list = [left_own] + left_others
    pieces = range(group_size)
    encT = enc_all.T.reshape(-1, group_size, attn_rows, enc_len)
    enc_rows = own_rows(encT)

    def take(which):
        return [piece[which * per_matrix : (which + 1) * per_matrix] for piece in left_list]

    cross_packs = [cross_pack] + cross_others
    cross_arrays = take(2) + take(3) + [enc_rows] + cross_packs + [enc_sum]
    g = group_size
    cross_picks = (
        (tuple((i, None) for i in pieces), tuple((2 * g + 1 + i, 1) for i in pieces)),
        (((2 * g, None),), ((3 * g + 1, 0),)),
        (((2 * g, None),), ((3 * g + 1, 1),)),
        (tuple((g + i, None) for i in pieces), tuple((2 * g + 1 + i, 0) for i in pieces)),
    )
    cross_grad = scatter_sum(
        lambda owners: run_attn_wgrad(
            owners, cross_picks, cross_arrays, g, per_matrix, attn_rows, features
        )
    )
    enc_own = lax.dynamic_slice_in_dim(enc_sum, group_pos * enc_piece, enc_piece, 1)
    encoder_grad = dot_nt(enc_own[0], cross_full[features : 2 * features]) + dot_nt(
        enc_own[1], cross_full[2 * features : 3 * features]
    )

    sums, stream_grad, gain_one = run_qkv_bwd(
        [self_pack] + self_others, self_full, stream, gains, self_in_grad
    )
    self_arrays = take(0) + take(1) + [sums[0], sums[1], sums[2]] + cross_packs
    self_picks = tuple(
        (tuple((i, None) for i in pieces), tuple((2 * g + m, i) for i in pieces)) for m in range(3)
    ) + ((tuple((g + i, None) for i in pieces), tuple((2 * g + 3 + i, 2) for i in pieces)),)
    self_grad = scatter_sum(
        lambda owners: run_attn_wgrad(
            owners, self_picks, self_arrays, g, per_matrix, attn_rows, features
        )
    )

    table_grad = jnp.dot(dist_grad, onehot_line, precision=lax.Precision.HIGHEST)
    table_flat = jnp.pad(table_grad.reshape(1, -1), ((0, 0), (0, features - table_grad.size)))
    small = jnp.concatenate([gain_one, gain_two, gain_three, table_flat], axis=0)
    for bit in range(shard_bits):
        small = small + swap(small, bit)
    step = 1
    while step < group_size:
        small = small + lax.ppermute(small, "seq", [(i, i ^ step) for i in range(group_size)])
        step *= 2
    return (
        output[None],
        stream_grad[None],
        encoder_grad[None],
        small[:3],
        small[3, : table_grad.size].reshape(table_grad.shape),
        self_grad,
        cross_grad,
        feed_grad,
    )


def solution(mesh):
    placed = (
        P("fsdp", "seq", None),
        P("fsdp", "seq", None),
        P("fsdp", None),
        P("fsdp", None),
        P("fsdp", None),
        P(None, "fsdp"),
        P(),
        P(),
        P("fsdp", None),
        P("fsdp", "seq", None),
    )
    return jax.shard_map(
        local,
        mesh=mesh,
        in_specs=placed,
        out_specs=(
            P("fsdp", "seq", None),
            P("fsdp", "seq", None),
            P("fsdp", "seq", None),
            P(),
            P(),
            P(("fsdp", "seq"), None),
            P(("fsdp", "seq"), None),
            P(("fsdp", "seq"), None),
        ),
        check_vma=False,
    )
```
